32 devices in a mesh: group: 2 (over x), fsdp: 8 (over z, y), ctx: 2 (over core).
Axes of the slice: x: 2, y: 2, z: 4, core: 2. Of those that a mesh axis runs over, the one named last changes fastest.
Arguments:
- normed: bfloat16 [16, 512, 8192], P(('group', 'fsdp'), 'ctx'), parts along dimension 0, may hold values from -6 to 6
- queries: bfloat16 [16, 512, 4096], P(('group', 'fsdp'), 'ctx'), parts along dimension 0, may hold values from -103 to 103
- key_weight: bfloat16 [8192, 512], P('fsdp'), may hold values from -0.0625 to 0.0625
- value_weight: bfloat16 [8192, 512], P('fsdp'), may hold values from -0.0625 to 0.0625
- doc_start: int32 [16], P(('group', 'fsdp')), parts along dimension 0, may hold values from 1 to 511
Outputs:
- attention: bfloat16 [16, 512, 4096], P(('group', 'fsdp'), 'ctx'), parts along dimension 0
The draws below stay inside these ranges and needn't reach their ends.
There are 2 independent parts, one for each index of `group`. The reference program is written for one: setup_inputs(seed, part) draws one part's arguments, and reference() takes and returns one part's arrays. A program takes and returns all parts, laid end to end along the dimension named above; an argument that names none is the same for every part. Nothing has to cross between parts.
Inputs may be any that keep to these rules, and one draw needn't show every extreme that they name: Rows before doc_start of a window belong to one document and the other rows to the next.
All inputs are finite; a program needn't handle non-finite values.
Results may differ from the reference program's by a relative error of at most 0.0055.
The reference program's roundings to bfloat16 on the way count: a program that leaves them out, or rounds other values in their place, can miss the bound.
Values may be sent and summed in bfloat16 or wider, within the bound.
A program may use at most 128 MiB of HBM per device.

```python
import jax
import jax.numpy as jnp
from jax import lax

D = 8192
HEAD_DIM = 128
GROUP = 8
KV_HEADS = 4
HEADS = 32
KVW = 512
QW = 4096
LENGTH = 512
WINDOWS = 8


def draw_queries(key, part):
    draw_shape = (WINDOWS, LENGTH, QW)
    values = jnp.clip(jax.random.normal(key, draw_shape, jnp.float32), -6.0, 6.0)
    return values.astype(jnp.bfloat16)


def touch_ends(result, key, low, largest):
    longest = result.shape.index(max(result.shape))
    spots = []
    for shift in (0, 1):
        where = [jax.random.randint(jax.random.fold_in(key, axis), (), 0, length) for axis, length in enumerate(result.shape)]
        where[longest] = (where[longest] + shift) % result.shape[longest]
        spots.append(tuple(where))
    return result.at[spots[0]].set(low).at[spots[1]].set(largest)


def block_scale(stream_key, extent, split, least, high):
    gain = 1.0
    for axis_at, shards_of in split:
        heights = jax.random.uniform(jax.random.fold_in(jax.random.fold_in(stream_key, 6), axis_at), (shards_of,), jnp.float32, least / len(split), high / len(split))
        gain = gain * jnp.repeat(jnp.exp(heights), extent[axis_at] // shards_of).reshape((-1,) + (1,) * (len(extent) - 1 - axis_at))
    return gain


def centred(own_key, dims, scale, limit, pieces=(), kind=jnp.bfloat16):
    array = jax.random.normal(own_key, dims, jnp.float32) * scale
    if len(pieces) > 0:
        array = block_scale(own_key, dims, pieces, -0.22, 0.18) * array
    return jnp.clip(array, min=-limit, max=limit).astype(kind)


def setup_inputs(seed: int = 0, part: int = 0) -> dict:
    seeds = jax.random.split(jax.random.key(seed), 6)
    part_splits = jax.random.split(jax.random.fold_in(seeds[5], part), 6)
    normed = centred(part_splits[0], (WINDOWS, LENGTH, D), 1.0, 6.0, ((0, 8), (1, 2)))
    queries = draw_queries(jax.random.fold_in(jax.random.fold_in(seeds[5], part), 71), part)
    key_weight = centred(seeds[2], (D, KVW), D ** -0.5, 0.0625, ((0, 8),))
    value_weight = centred(seeds[3], (D, KVW), D ** -0.5, 0.0625, ((0, 8),))
    doc_start = touch_ends(jax.random.randint(part_splits[4], (WINDOWS,), 1, LENGTH), jax.random.fold_in(part_splits[4], 1), 1, LENGTH - 1).astype(jnp.int32)
    return {"normed": normed, "queries": queries, "key_weight": key_weight, "value_weight": value_weight, "doc_start": doc_start}


theta_base = 500000.0
masked_score = -1.0e30


def rotate(values, positions):
    head_width = values.shape[-1]
    half_width = head_width // 2
    frequency = theta_base ** (-jnp.arange(half_width, dtype=jnp.float32) * 2.0 / head_width)
    angles = positions.astype(jnp.float32)[:, None] * frequency[None, :]
    cosine = jnp.cos(angles)[:, None, :]
    sine_part = jnp.sin(angles)[:, None, :]
    first_half = values[..., :half_width]
    second_half = values[..., half_width:]
    return jnp.concatenate([first_half * cosine - second_half * sine_part, second_half * cosine + first_half * sine_part], axis=-1)


def reference(normed, queries, key_weight, value_weight, doc_start):
    windows, length, model_width = normed.shape
    flattened = normed.reshape(windows * length, model_width)
    positions = jnp.arange(length, dtype=jnp.int32)
    key_proj = jnp.dot(flattened, key_weight, preferred_element_type=jnp.float32)
    value_proj = jnp.dot(flattened, value_weight, preferred_element_type=jnp.float32)
    key_heads = rotate(key_proj.reshape(windows, length, KV_HEADS, HEAD_DIM), positions).astype(jnp.bfloat16)
    value_heads = value_proj.astype(jnp.bfloat16).reshape(windows, length, KV_HEADS, HEAD_DIM)
    query_heads = rotate(queries.astype(jnp.float32).reshape(windows, length, HEADS, HEAD_DIM), positions)
    query_heads = query_heads.astype(jnp.bfloat16).reshape(windows, length, KV_HEADS, GROUP, HEAD_DIM)

    def one_window(operands):
        query_block, key_block, value_block, doc_bound = operands
        scores = jnp.einsum("rkgd,skd->kgrs", query_block.astype(jnp.float32), key_block.astype(jnp.float32)) * HEAD_DIM ** -0.5
        before_query = positions[None, :] <= positions[:, None]
        same_document = (positions[None, :] >= doc_bound) | (positions[:, None] < doc_bound)
        visible = before_query & same_document
        scores = jnp.where(visible, scores, masked_score)
        row_max = jnp.max(scores, axis=-1, keepdims=True)
        weights = jnp.where(visible, jnp.exp(scores - row_max), 0.0)
        denominator = jnp.sum(weights, axis=-1)
        context = jnp.einsum("kgrs,skd->rkgd", weights.astype(jnp.bfloat16).astype(jnp.float32), value_block.astype(jnp.float32))
        context = context / jnp.transpose(denominator, (2, 0, 1))[..., None]
        return context.astype(jnp.bfloat16).reshape(length, HEADS * HEAD_DIM)

    return lax.map(one_window, (query_heads, key_heads, value_heads, doc_start))
```

```python
import functools

import jax
import jax.numpy as jnp
import numpy as np
from jax import lax
from jax.experimental import pallas as pl
from jax.experimental.pallas import tpu as pltpu
from jax.sharding import PartitionSpec as P

HEAD_DIM = 128
GROUP = 8
THETA = 500000.0
MASKED = -1e30
MESH = pl.DeviceIdType.MESH
PHASES = 2


def rotary_tables(length):
    half = HEAD_DIM // 2
    exponent = -np.arange(half, dtype=np.float32) * np.float32(2.0) / np.float32(HEAD_DIM)
    frequency = np.power(np.float32(THETA), exponent, dtype=np.float32)
    angles = np.arange(length, dtype=np.float32)[:, None] * frequency[None, :]
    cosine, sine = np.cos(angles).astype(np.float32), np.sin(angles).astype(np.float32)
    return np.concatenate([cosine, cosine], 1), np.concatenate([-sine, sine], 1)


def kernel(
    groups, shards, doc_ref, normed_ref, queries_ref, key_ref, value_ref, cos_hbm, sin_hbm, out_ref,
    wbuf, xbuf, qbuf, obuf, acc, kbuf, vbuf, bias, cos_ref, sin_ref,
    load_sem, recv_sem, z_sem, y_sem, x_sem, pair_send, pair_recv, out_sem, out_send, out_recv,
):
    twins = groups == 2
    ny = 2 if twins else 1
    nz = shards // ny
    parts = 4 if twins else 1
    zparts = 3 if twins else 1
    g, f, c = lax.axis_index("group"), lax.axis_index("fsdp"), lax.axis_index("ctx")
    z, y = f // ny, f % ny
    own_rows, depth = normed_ref.shape[1], key_ref.shape[0]
    length = 2 * own_rows
    piece_rows = depth // parts
    half_cols = queries_ref.shape[2] // 2
    pair = (g, f, 1 - c)
    up, down = (g, f + ny, c), (g, f - ny, c)
    if twins:
        y_dev, x_dev = (g, z * 2 + 1 - y, c), (1 - g, f, c)

    def shard(zs, ys):
        return zs * ny + ys

    def part(j):
        return g * (parts - 1) + j * (1 - 2 * g) if twins else 0

    def piece(h, s, q):
        return wbuf.at[h, s, pl.ds(pl.multiple_of(q * piece_rows, piece_rows), piece_rows), :]

    def copy(h, s, q, send_sem, device):
        ref = piece(h, s, q)
        return pltpu.make_async_remote_copy(
            src_ref=ref, dst_ref=ref, send_sem=send_sem, recv_sem=recv_sem.at[h, s, q],
            device_id=device, device_id_type=MESH,
        )

    def z_copy(h, zs, j, way):
        q = part(j)
        return copy(h, shard(zs, y), q, z_sem.at[way, h, zs, j], up if way == 0 else down)

    def y_copy(h, zs, j):
        return copy(h, shard(zs, y), part(j), y_sem.at[h, zs, j], y_dev)

    def x_copy(h, zs, ys, j, slot):
        return copy(h, shard(zs, ys), part(j), x_sem.at[h, zs, slot], x_dev)

    def wait_piece(h, s, j):
        q = part(j)
        copy(h, s, q, recv_sem.at[h, s, q], pair).wait_recv()

    head_cols = [pl.ds(pl.multiple_of((2 * c + h) * HEAD_DIM, HEAD_DIM), HEAD_DIM) for h in range(PHASES)]
    weight_loads = []
    for h in range(PHASES):
        weight_loads.append([
            pltpu.make_async_copy(key_ref.at[:, head_cols[h]], wbuf.at[h, f, :, pl.ds(0, HEAD_DIM)], load_sem.at[2 * h]),
            pltpu.make_async_copy(value_ref.at[:, head_cols[h]], wbuf.at[h, f, :, pl.ds(HEAD_DIM, HEAD_DIM)], load_sem.at[2 * h + 1]),
        ])
    own = pl.ds(pl.multiple_of(c * own_rows, own_rows), own_rows)
    other = pl.ds(pl.multiple_of((1 - c) * own_rows, own_rows), own_rows)
    my_cols = pl.ds(pl.multiple_of(c * half_cols, half_cols), half_cols)
    other_cols = pl.ds(pl.multiple_of((1 - c) * half_cols, half_cols), half_cols)
    other_loads = [
        pltpu.make_async_copy(normed_ref.at[0], xbuf.at[own, :], load_sem.at[4]),
        pltpu.make_async_copy(queries_ref.at[0, :, my_cols], qbuf.at[own, :], load_sem.at[5]),
        pltpu.make_async_copy(cos_hbm, cos_ref, load_sem.at[6]),
        pltpu.make_async_copy(sin_hbm, sin_ref, load_sem.at[7]),
    ]
    for loads in weight_loads:
        for load in loads:
            load.start()

    barrier = pltpu.get_barrier_semaphore()
    pl.semaphore_signal(barrier, inc=1, device_id=pair, device_id_type=MESH)
    if twins:
        pl.semaphore_signal(barrier, inc=1, device_id=y_dev, device_id_type=MESH)
        pl.semaphore_signal(barrier, inc=1, device_id=x_dev, device_id_type=MESH)

    @pl.when(z < nz - 1)
    def _():
        pl.semaphore_signal(barrier, inc=1, device_id=up, device_id_type=MESH)

    @pl.when(z > 0)
    def _():
        pl.semaphore_signal(barrier, inc=1, device_id=down, device_id_type=MESH)

    line_peers = jnp.where(z > 0, 1, 0) + jnp.where(z < nz - 1, 1, 0)
    pl.semaphore_wait(barrier, (3 if twins else 1) + line_peers)

    def send_own(h):
        for load in weight_loads[h]:
            load.wait()
        for j in range(parts):
            if j < zparts:
                @pl.when(z < nz - 1)
                def _():
                    z_copy(h, z, j, 0).start()

                @pl.when(z > 0)
                def _():
                    z_copy(h, z, j, 1).start()
            if twins:
                y_copy(h, z, j).start()

    def each_way(d, action):
        @pl.when(z - d >= 0)
        def _():
            action(z - d, 0)

        @pl.when(z + d < nz)
        def _():
            action(z + d, 1)

    def passes_on(way):
        return z < nz - 1 if way == 0 else z > 0

    def forward_z(h, d):
        for j in range(zparts):
            def one(zs, way, j=j):
                wait_piece(h, shard(zs, y), j)

                @pl.when(passes_on(way))
                def _():
                    z_copy(h, zs, j, way).start()

                if twins:
                    if j < 2:
                        y_copy(h, zs, j).start()
                    if j == 0:
                        x_copy(h, zs, y, 0, 0).start()

            each_way(d, one)

    def forward_y(h, d):
        for j in range(2):
            def one(zs, way, j=j):
                wait_piece(h, shard(zs, 1 - y), j)
                x_copy(h, zs, 1 - y, j, 1 + j).start()

            each_way(d, one)

    def drain_sends(h, d):
        def one(zs, way):
            for j in range(zparts):
                @pl.when(passes_on(way))
                def _():
                    z_copy(h, zs, j, way).wait_send()

            if twins:
                for j in range(2):
                    y_copy(h, zs, j).wait_send()
                    x_copy(h, zs, 1 - y, j, 1 + j).wait_send()
                x_copy(h, zs, y, 0, 0).wait_send()

        each_way(d, one)

    def drain_own(h):
        for j in range(parts):
            if j < zparts:
                @pl.when(z < nz - 1)
                def _():
                    z_copy(h, z, j, 0).wait_send()

                @pl.when(z > 0)
                def _():
                    z_copy(h, z, j, 1).wait_send()
            if twins:
                y_copy(h, z, j).wait_send()

    def add_shard(h, s):
        columns = pl.ds(pl.multiple_of(s * depth, depth), depth)

        def tile(t, carry):
            rows = pl.ds(pl.multiple_of(t * 256, 256), 256)
            acc[h, rows, :] += jnp.dot(xbuf[rows, columns], wbuf[h, s], preferred_element_type=jnp.float32)
            return carry

        lax.fori_loop(0, length // 256, tile, 0)

    def add_same(h, d):
        def one(zs, way):
            if twins:
                wait_piece(h, shard(zs, y), 3)
            add_shard(h, shard(zs, y))

        each_way(d, one)

    def add_other(h, d):
        def one(zs, way):
            for j in range(2, 4):
                wait_piece(h, shard(zs, 1 - y), j)
            add_shard(h, shard(zs, 1 - y))

        each_way(d, one)

    def add_beside(h):
        for j in range(4):
            wait_piece(h, shard(z, 1 - y), j)
        add_shard(h, shard(z, 1 - y))

    def rotated(u, rows):
        return (u * cos_ref[rows, :] + pltpu.roll(u, HEAD_DIM // 2, 1) * sin_ref[rows, :]).astype(jnp.bfloat16)

    def rotate_queries():
        for load in other_loads[1:]:
            load.wait()
        query_copy.wait_recv()

        def head(i, carry):
            cols = pl.ds(pl.multiple_of(i * HEAD_DIM, HEAD_DIM), HEAD_DIM)

            def tile(t, carry):
                rows = pl.ds(pl.multiple_of(t * 128, 128), 128)
                qbuf[rows, cols] = rotated(qbuf[rows, cols].astype(jnp.float32), rows)
                return carry

            return lax.fori_loop(0, length // 128, tile, carry)

        lax.fori_loop(0, half_cols // HEAD_DIM, head, 0)

    def make_bias():
        first = doc_ref[0]
        row = lax.broadcasted_iota(jnp.int32, (length, length), 0)
        col = lax.broadcasted_iota(jnp.int32, (length, length), 1)
        visible = (col <= row) & ((col >= first) | (row < first))
        bias[...] = jnp.where(visible, 0.0, MASKED)

    def finish_heads(h):
        def tile(t, carry):
            rows = pl.ds(pl.multiple_of(t * 128, 128), 128)
            kbuf[h, rows, :] = rotated(acc[h, rows, :HEAD_DIM], rows)
            vbuf[h, rows, :] = acc[h, rows, HEAD_DIM:].astype(jnp.bfloat16)
            return carry

        lax.fori_loop(0, length // 128, tile, 0)

    factor = HEAD_DIM ** -0.5 * 1.4426950408889634

    def attend(h, first, count):
        def head(i, carry):
            cols = pl.ds(pl.multiple_of((h * GROUP + i) * HEAD_DIM, HEAD_DIM), HEAD_DIM)
            for block in range(2):
                rows = slice(block * own_rows, (block + 1) * own_rows)
                keys = (block + 1) * own_rows
                scores = lax.dot_general(
                    qbuf[rows, cols], kbuf[h, :keys, :], (((1,), (1,)), ((), ())),
                    preferred_element_type=jnp.float32,
                ) * factor + bias[rows, :keys]
                probs = jnp.exp2(scores - jnp.max(scores, axis=1, keepdims=True))
                total = jnp.sum(probs, axis=1, keepdims=True)
                mixed = jnp.dot(probs.astype(jnp.bfloat16), vbuf[h, :keys, :], preferred_element_type=jnp.float32)
                obuf[rows, cols] = (mixed / total).astype(jnp.bfloat16)
            return carry

        lax.fori_loop(first, first + count, head, 0)

    def out_copies(h):
        width = GROUP * HEAD_DIM
        source = pl.ds(h * width, width)
        target = out_ref.at[0, :, pl.ds(pl.multiple_of((2 * c + h) * width, width), width)]
        return (
            pltpu.make_async_copy(obuf.at[own, source], target, out_sem.at[h]),
            pltpu.make_async_remote_copy(
                src_ref=obuf.at[other, source], dst_ref=target, send_sem=out_send.at[h],
                recv_sem=out_recv.at[h], device_id=pair, device_id_type=MESH,
            ),
        )

    def send_out(h):
        for one in out_copies(h):
            one.start()

    send_own(0)
    query_copy = pltpu.make_async_remote_copy(
        src_ref=queries_ref.at[0, :, other_cols], dst_ref=qbuf.at[own, :], send_sem=pair_send.at[0],
        recv_sem=pair_recv.at[0], device_id=pair, device_id_type=MESH,
    )
    normed_copy = pltpu.make_async_remote_copy(
        src_ref=normed_ref.at[0], dst_ref=xbuf.at[own, :], send_sem=pair_send.at[1],
        recv_sem=pair_recv.at[1], device_id=pair, device_id_type=MESH,
    )
    for load in other_loads:
        load.start()
    query_copy.start()
    normed_copy.start()
    acc[...] = jnp.zeros_like(acc)
    make_bias()

    def wait_normed():
        other_loads[0].wait()
        normed_copy.wait_recv()

    if twins:
        forward_z(0, 1)
        rotate_queries()
        forward_z(0, 2)
        forward_y(0, 1)
        send_own(1)
        forward_z(0, 3)
        forward_y(0, 2)
        wait_normed()
        add_shard(0, f)
        add_beside(0)
        add_same(0, 1)
        forward_y(0, 3)
        forward_z(1, 1)
        add_same(0, 2)
        add_other(0, 1)
        forward_z(1, 2)
        forward_y(1, 1)
        add_same(0, 3)
        add_other(0, 2)
        add_other(0, 3)
        finish_heads(0)
        attend(0, 0, 2)
        forward_z(1, 3)
        forward_y(1, 2)
        attend(0, 2, 2)
        add_shard(1, f)
        add_beside(1)
        forward_y(1, 3)
        attend(0, 4, 4)
        send_out(0)
        for d in (1, 2, 3):
            add_same(1, d)
            add_other(1, d)
        finish_heads(1)
    else:
        rotate_queries()
        send_own(1)
        wait_normed()
        for h in range(PHASES):
            add_shard(h, f)

            def step(d, carry, h=h):
                forward_z(h, d)
                add_same(h, d)
                return carry

            lax.fori_loop(1, nz, step, 0)
            finish_heads(h)
            if h == 0:
                attend(0, 0, GROUP)
                send_out(0)
    attend(1, 0, GROUP)
    send_out(1)

    for h in range(PHASES):
        drain_own(h)

        def drain(d, carry, h=h):
            drain_sends(h, d)
            return carry

        lax.fori_loop(1, nz, drain, 0)
    query_copy.wait_send()
    normed_copy.wait_send()
    for h in range(PHASES):
        local, remote = out_copies(h)
        local.wait()
        remote.wait()


def body(groups, shards, normed, queries, key_weight, value_weight, doc_start):
    _, rows, width = normed.shape
    depth = key_weight.shape[0]
    query_cols = queries.shape[2]
    length = 2 * rows
    nz = shards // 2 if groups == 2 else shards
    parts = 4 if groups == 2 else 1
    cosine, sine = rotary_tables(length)
    dma = pltpu.SemaphoreType.DMA
    hbm = pl.BlockSpec(memory_space=pl.ANY)
    return pl.pallas_call(
        functools.partial(kernel, groups, shards),
        out_shape=jax.ShapeDtypeStruct((1, rows, query_cols), jnp.bfloat16),
        in_specs=[pl.BlockSpec(memory_space=pltpu.SMEM)] + [hbm] * 6,
        out_specs=hbm,
        scratch_shapes=[
            pltpu.VMEM((PHASES, shards, depth, 2 * HEAD_DIM), jnp.bfloat16),
            pltpu.VMEM((length, width), jnp.bfloat16),
            pltpu.VMEM((length, query_cols // 2), jnp.bfloat16),
            pltpu.VMEM((length, query_cols // 2), jnp.bfloat16),
            pltpu.VMEM((PHASES, length, 2 * HEAD_DIM), jnp.float32),
            pltpu.VMEM((PHASES, length, HEAD_DIM), jnp.bfloat16),
            pltpu.VMEM((PHASES, length, HEAD_DIM), jnp.bfloat16),
            pltpu.VMEM((length, length), jnp.float32),
            pltpu.VMEM((length, HEAD_DIM), jnp.float32),
            pltpu.VMEM((length, HEAD_DIM), jnp.float32),
            dma((8,)),
            dma((PHASES, shards, parts)),
            dma((2, PHASES, nz, 3)),
            dma((PHASES, nz, 4)),
            dma((PHASES, nz, 3)),
            dma((2,)),
            dma((2,)),
            dma((2,)),
            dma((2,)),
            dma((2,)),
        ],
        compiler_params=pltpu.CompilerParams(
            collective_id=0, has_side_effects=True, vmem_limit_bytes=56 * 1024 * 1024
        ),
    )(doc_start, normed, queries, key_weight, value_weight, jnp.asarray(cosine), jnp.asarray(sine))


def solution(mesh):
    placed = (
        P(("group", "fsdp"), "ctx", None),
        P(("group", "fsdp"), "ctx", None),
        P("fsdp", None),
        P("fsdp", None),
        P(("group", "fsdp")),
    )
    return jax.shard_map(
        functools.partial(body, mesh.shape["group"], mesh.shape["fsdp"]),
        mesh=mesh,
        in_specs=placed,
        out_specs=P(("group", "fsdp"), "ctx", None),
        check_vma=False,
    )
```

```python
import functools

import jax
import jax.numpy as jnp
import numpy as np
from jax import lax
from jax.experimental import pallas as pl
from jax.experimental.pallas import tpu as pltpu
from jax.sharding import PartitionSpec as P

HEAD_DIM = 128
GROUP = 8
THETA = 500000.0
MASKED = -1e30
MESH = pl.DeviceIdType.MESH
PHASES = 2
OUT_GROUPS = 4


def rotary_tables(length):
    half = HEAD_DIM // 2
    exponent = -np.arange(half, dtype=np.float32) * np.float32(2.0) / np.float32(HEAD_DIM)
    frequency = np.power(np.float32(THETA), exponent, dtype=np.float32)
    angles = np.arange(length, dtype=np.float32)[:, None] * frequency[None, :]
    cosine, sine = np.cos(angles).astype(np.float32), np.sin(angles).astype(np.float32)
    return np.concatenate([cosine, cosine], 1), np.concatenate([-sine, sine], 1)


def kernel(
    groups, shards, doc_ref, normed_ref, queries_ref, key_ref, value_ref, cos_hbm, sin_hbm, out_ref,
    wbuf, xbuf, qbuf, obuf, pbuf, inverse, acc, kbuf, vbuf, bias, cos_ref, sin_ref,
    load_sem, recv_sem, z_sem, y_sem, x_sem, pair_send, pair_recv, out_sem, out_send, out_recv,
):
    twins = groups == 2
    ny = 2 if twins else 1
    nz = shards // ny
    parts = 4 if twins else 1
    zparts = 3 if twins else 1
    g, f, c = lax.axis_index("group"), lax.axis_index("fsdp"), lax.axis_index("ctx")
    z, y = f // ny, f % ny
    own_rows, depth = normed_ref.shape[1], key_ref.shape[0]
    length = 2 * own_rows
    piece_rows = depth // parts
    half_cols = queries_ref.shape[2] // 2
    pair = (g, f, 1 - c)
    up, down = (g, f + ny, c), (g, f - ny, c)
    if twins:
        y_dev, x_dev = (g, z * 2 + 1 - y, c), (1 - g, f, c)

    def shard(zs, ys):
        return zs * ny + ys

    def part(j):
        return g * (parts - 1) + j * (1 - 2 * g) if twins else 0

    def piece(h, s, q):
        return wbuf.at[h, s, pl.ds(pl.multiple_of(q * piece_rows, piece_rows), piece_rows), :]

    def copy(h, s, q, send_sem, device):
        ref = piece(h, s, q)
        return pltpu.make_async_remote_copy(
            src_ref=ref, dst_ref=ref, send_sem=send_sem, recv_sem=recv_sem.at[h, s, q],
            device_id=device, device_id_type=MESH,
        )

    def z_copy(h, zs, j, way):
        q = part(j)
        return copy(h, shard(zs, y), q, z_sem.at[way, h, zs, j], up if way == 0 else down)

    def y_copy(h, zs, j):
        return copy(h, shard(zs, y), part(j), y_sem.at[h, zs, j], y_dev)

    def x_copy(h, zs, ys, j, slot):
        return copy(h, shard(zs, ys), part(j), x_sem.at[h, zs, slot], x_dev)

    def wait_piece(h, s, j):
        q = part(j)
        copy(h, s, q, recv_sem.at[h, s, q], pair).wait_recv()

    head_cols = pl.ds(pl.multiple_of(c * 2 * HEAD_DIM, 2 * HEAD_DIM), 2 * HEAD_DIM)
    weight_loads = [
        pltpu.make_async_copy(ref.at[:, head_cols], wbuf.at[h, f], load_sem.at[h])
        for h, ref in enumerate((key_ref, value_ref))
    ]
    own = pl.ds(pl.multiple_of(c * own_rows, own_rows), own_rows)
    other = pl.ds(pl.multiple_of((1 - c) * own_rows, own_rows), own_rows)
    my_cols = pl.ds(pl.multiple_of(c * half_cols, half_cols), half_cols)
    other_cols = pl.ds(pl.multiple_of((1 - c) * half_cols, half_cols), half_cols)
    other_loads = [
        pltpu.make_async_copy(normed_ref.at[0], xbuf.at[own, :], load_sem.at[2]),
        pltpu.make_async_copy(queries_ref.at[0, :, my_cols], qbuf.at[own, :], load_sem.at[3]),
        pltpu.make_async_copy(cos_hbm, cos_ref, load_sem.at[4]),
        pltpu.make_async_copy(sin_hbm, sin_ref, load_sem.at[5]),
    ]
    for load in weight_loads:
        load.start()

    barrier = pltpu.get_barrier_semaphore()
    pl.semaphore_signal(barrier, inc=1, device_id=pair, device_id_type=MESH)
    if twins:
        pl.semaphore_signal(barrier, inc=1, device_id=y_dev, device_id_type=MESH)
        pl.semaphore_signal(barrier, inc=1, device_id=x_dev, device_id_type=MESH)

    @pl.when(z < nz - 1)
    def _():
        pl.semaphore_signal(barrier, inc=1, device_id=up, device_id_type=MESH)

    @pl.when(z > 0)
    def _():
        pl.semaphore_signal(barrier, inc=1, device_id=down, device_id_type=MESH)

    line_peers = jnp.where(z > 0, 1, 0) + jnp.where(z < nz - 1, 1, 0)
    pl.semaphore_wait(barrier, (3 if twins else 1) + line_peers)

    def sends_beside(h, j):
        return twins and (h != 0 or j != 3)

    def send_own(h):
        weight_loads[h].wait()
        for j in range(parts):
            if j < zparts:
                @pl.when(z < nz - 1)
                def _():
                    z_copy(h, z, j, 0).start()

                @pl.when(z > 0)
                def _():
                    z_copy(h, z, j, 1).start()
            if sends_beside(h, j):
                y_copy(h, z, j).start()

    def each_way(d, action):
        @pl.when(z - d >= 0)
        def _():
            action(z - d, 0)

        @pl.when(z + d < nz)
        def _():
            action(z + d, 1)

    def passes_on(way):
        return z < nz - 1 if way == 0 else z > 0

    def forward_z(h, d):
        for j in range(zparts):
            def one(zs, way, j=j):
                wait_piece(h, shard(zs, y), j)

                @pl.when(passes_on(way))
                def _():
                    z_copy(h, zs, j, way).start()

                if twins:
                    if j < 2:
                        y_copy(h, zs, j).start()
                    if j == 0:
                        x_copy(h, zs, y, 0, 0).start()

            each_way(d, one)

    def forward_y(h, d):
        for j in range(2):
            def one(zs, way, j=j):
                wait_piece(h, shard(zs, 1 - y), j)
                x_copy(h, zs, 1 - y, j, 1 + j).start()

            each_way(d, one)

    def drain_sends(h, d):
        def one(zs, way):
            for j in range(zparts):
                @pl.when(passes_on(way))
                def _():
                    z_copy(h, zs, j, way).wait_send()

            if twins:
                for j in range(2):
                    y_copy(h, zs, j).wait_send()
                    x_copy(h, zs, 1 - y, j, 1 + j).wait_send()
                x_copy(h, zs, y, 0, 0).wait_send()

        each_way(d, one)

    def drain_own(h):
        for j in range(parts):
            if j < zparts:
                @pl.when(z < nz - 1)
                def _():
                    z_copy(h, z, j, 0).wait_send()

                @pl.when(z > 0)
                def _():
                    z_copy(h, z, j, 1).wait_send()
            if sends_beside(h, j):
                y_copy(h, z, j).wait_send()
        if twins and h == 0:
            x_copy(h, z, 1 - y, 0, 0).wait_send()

    def add_shard(h, s):
        columns = pl.ds(pl.multiple_of(s * depth, depth), depth)

        def tile(t, carry):
            rows = pl.ds(pl.multiple_of(t * 256, 256), 256)
            acc[h, rows, :] += jnp.dot(xbuf[rows, columns], wbuf[h, s], preferred_element_type=jnp.float32)
            return carry

        lax.fori_loop(0, length // 256, tile, 0)

    def add_same(h, d):
        def one(zs, way):
            if twins:
                wait_piece(h, shard(zs, y), 3)
            add_shard(h, shard(zs, y))

        each_way(d, one)

    def add_other(h, d):
        def one(zs, way):
            for j in range(2, 4):
                wait_piece(h, shard(zs, 1 - y), j)
            add_shard(h, shard(zs, 1 - y))

        each_way(d, one)

    def forward_beside():
        wait_piece(0, shard(z, 1 - y), 0)
        x_copy(0, z, 1 - y, 0, 0).start()

    def add_beside(h):
        for j in range(1 if h == 0 else 0, 4):
            wait_piece(h, shard(z, 1 - y), j)
        add_shard(h, shard(z, 1 - y))

    def rotated(u, rows):
        return (u * cos_ref[rows, :] + pltpu.roll(u, HEAD_DIM // 2, 1) * sin_ref[rows, :]).astype(jnp.bfloat16)

    def rotate_queries():
        for load in other_loads[1:]:
            load.wait()
        query_copy.wait_recv()

        def head(i, carry):
            cols = pl.ds(pl.multiple_of(i * HEAD_DIM, HEAD_DIM), HEAD_DIM)

            def tile(t, carry):
                rows = pl.ds(pl.multiple_of(t * 128, 128), 128)
                qbuf[rows, cols] = rotated(qbuf[rows, cols].astype(jnp.float32), rows)
                return carry

            return lax.fori_loop(0, length // 128, tile, carry)

        lax.fori_loop(0, half_cols // HEAD_DIM, head, 0)

    def make_bias():
        first = doc_ref[0]
        row = lax.broadcasted_iota(jnp.int32, (length, length), 0)
        col = lax.broadcasted_iota(jnp.int32, (length, length), 1)
        visible = (col <= row) & ((col >= first) | (row < first))
        bias[...] = jnp.where(visible, 0.0, MASKED)

    def finish_keys():
        def tile(t, carry):
            rows = pl.ds(pl.multiple_of(t * 128, 128), 128)
            for h in range(2):
                kbuf[h, rows, :] = rotated(acc[0, rows, h * HEAD_DIM:(h + 1) * HEAD_DIM], rows)
            return carry

        lax.fori_loop(0, length // 128, tile, 0)

    factor = HEAD_DIM ** -0.5 * 1.4426950408889634

    def weigh(first, count):
        h = first // GROUP

        def head(i, carry):
            cols = pl.ds(pl.multiple_of(i * HEAD_DIM, HEAD_DIM), HEAD_DIM)
            for block in range(2):
                rows = slice(block * own_rows, (block + 1) * own_rows)
                keys = (block + 1) * own_rows
                scores = lax.dot_general(
                    qbuf[rows, cols], kbuf[h, :keys, :], (((1,), (1,)), ((), ())),
                    preferred_element_type=jnp.float32,
                ) * factor + bias[rows, :keys]
                probs = jnp.exp2(scores - jnp.max(scores, axis=1, keepdims=True))
                total = jnp.sum(probs, axis=1, keepdims=True)
                pbuf[i, rows, :keys] = probs.astype(jnp.bfloat16)
                inverse[i, rows, :] = jnp.broadcast_to(1.0 / total, (own_rows, HEAD_DIM))
            return carry

        lax.fori_loop(first, first + count, head, 0)

    def mix(first, count):
        h = first // GROUP

        def head(i, carry):
            cols = pl.ds(pl.multiple_of(i * HEAD_DIM, HEAD_DIM), HEAD_DIM)
            for block in range(2):
                rows = slice(block * own_rows, (block + 1) * own_rows)
                keys = (block + 1) * own_rows
                mixed = jnp.dot(
                    pbuf[i, rows, :keys], vbuf[:keys, h * HEAD_DIM:(h + 1) * HEAD_DIM],
                    preferred_element_type=jnp.float32,
                )
                obuf[rows, cols] = (mixed * inverse[i, rows, :]).astype(jnp.bfloat16)
            return carry

        lax.fori_loop(first, first + count, head, 0)

    def out_copies(h):
        width = half_cols // OUT_GROUPS
        source = pl.ds(h * width, width)
        target = out_ref.at[0, :, pl.ds(pl.multiple_of(c * half_cols + h * width, width), width)]
        return (
            pltpu.make_async_copy(obuf.at[own, source], target, out_sem.at[h]),
            pltpu.make_async_remote_copy(
                src_ref=obuf.at[other, source], dst_ref=target, send_sem=out_send.at[h],
                recv_sem=out_recv.at[h], device_id=pair, device_id_type=MESH,
            ),
        )

    def send_out(h):
        for one in out_copies(h):
            one.start()

    send_own(0)
    query_copy = pltpu.make_async_remote_copy(
        src_ref=queries_ref.at[0, :, other_cols], dst_ref=qbuf.at[own, :], send_sem=pair_send.at[0],
        recv_sem=pair_recv.at[0], device_id=pair, device_id_type=MESH,
    )
    normed_copy = pltpu.make_async_remote_copy(
        src_ref=normed_ref.at[0], dst_ref=xbuf.at[own, :], send_sem=pair_send.at[1],
        recv_sem=pair_recv.at[1], device_id=pair, device_id_type=MESH,
    )
    for load in other_loads:
        load.start()
    query_copy.start()
    normed_copy.start()
    acc[...] = jnp.zeros_like(acc)
    make_bias()

    def wait_normed():
        other_loads[0].wait()
        normed_copy.wait_recv()

    if twins:
        forward_z(0, 1)
        rotate_queries()
        forward_beside()
        forward_z(0, 2)
        forward_y(0, 1)
        send_own(1)
        forward_y(0, 2)
        forward_z(0, 3)
        wait_normed()
        add_shard(0, f)
        add_beside(0)
        add_same(0, 1)
        forward_y(0, 3)
        add_same(0, 2)
        add_other(0, 1)
        forward_z(1, 1)
        add_same(0, 3)
        add_other(0, 2)
        add_other(0, 3)
        finish_keys()
        weigh(0, 2)
        forward_z(1, 2)
        weigh(2, 2)
        forward_y(1, 1)
        weigh(4, 2)
        add_shard(1, f)
        forward_y(1, 2)
        weigh(6, 2)
        forward_z(1, 3)
        weigh(8, 2)
        forward_y(1, 3)
        weigh(10, 6)
        add_beside(1)
        for d in (1, 2, 3):
            add_same(1, d)
            add_other(1, d)
    else:
        rotate_queries()
        send_own(1)
        wait_normed()
        for h in range(PHASES):
            add_shard(h, f)

            def step(d, carry, h=h):
                forward_z(h, d)
                add_same(h, d)
                return carry

            lax.fori_loop(1, nz, step, 0)
            if h == 0:
                finish_keys()
                weigh(0, 8)
                weigh(8, 8)
    vbuf[...] = acc[1].astype(jnp.bfloat16)
    heads = 2 * GROUP // OUT_GROUPS
    for group in range(OUT_GROUPS):
        mix(group * heads, heads)
        send_out(group)

    for h in range(PHASES):
        drain_own(h)

        def drain(d, carry, h=h):
            drain_sends(h, d)
            return carry

        lax.fori_loop(1, nz, drain, 0)
    query_copy.wait_send()
    normed_copy.wait_send()
    for group in range(OUT_GROUPS):
        local, remote = out_copies(group)
        local.wait()
        remote.wait()


def body(groups, shards, normed, queries, key_weight, value_weight, doc_start):
    _, rows, width = normed.shape
    depth = key_weight.shape[0]
    query_cols = queries.shape[2]
    length = 2 * rows
    nz = shards // 2 if groups == 2 else shards
    parts = 4 if groups == 2 else 1
    cosine, sine = rotary_tables(length)
    dma = pltpu.SemaphoreType.DMA
    hbm = pl.BlockSpec(memory_space=pl.ANY)
    return pl.pallas_call(
        functools.partial(kernel, groups, shards),
        out_shape=jax.ShapeDtypeStruct((1, rows, query_cols), jnp.bfloat16),
        in_specs=[pl.BlockSpec(memory_space=pltpu.SMEM)] + [hbm] * 6,
        out_specs=hbm,
        scratch_shapes=[
            pltpu.VMEM((PHASES, shards, depth, 2 * HEAD_DIM), jnp.bfloat16),
            pltpu.VMEM((length, width), jnp.bfloat16),
            pltpu.VMEM((length, query_cols // 2), jnp.bfloat16),
            pltpu.VMEM((length, query_cols // 2), jnp.bfloat16),
            pltpu.VMEM((2 * GROUP, length, length), jnp.bfloat16),
            pltpu.VMEM((2 * GROUP, length, HEAD_DIM), jnp.float32),
            pltpu.VMEM((PHASES, length, 2 * HEAD_DIM), jnp.float32),
            pltpu.VMEM((2, length, HEAD_DIM), jnp.bfloat16),
            pltpu.VMEM((length, 2 * HEAD_DIM), jnp.bfloat16),
            pltpu.VMEM((length, length), jnp.float32),
            pltpu.VMEM((length, HEAD_DIM), jnp.float32),
            pltpu.VMEM((length, HEAD_DIM), jnp.float32),
            dma((6,)),
            dma((PHASES, shards, parts)),
            dma((2, PHASES, nz, 3)),
            dma((PHASES, nz, 4)),
            dma((PHASES, nz, 3)),
            dma((2,)),
            dma((2,)),
            dma((OUT_GROUPS,)),
            dma((OUT_GROUPS,)),
            dma((OUT_GROUPS,)),
        ],
        compiler_params=pltpu.CompilerParams(
            collective_id=0, has_side_effects=True, vmem_limit_bytes=56 * 1024 * 1024
        ),
    )(doc_start, normed, queries, key_weight, value_weight, jnp.asarray(cosine), jnp.asarray(sine))


def solution(mesh):
    placed = (
        P(("group", "fsdp"), "ctx", None),
        P(("group", "fsdp"), "ctx", None),
        P("fsdp", None),
        P("fsdp", None),
        P(("group", "fsdp")),
    )
    return jax.shard_map(
        functools.partial(body, mesh.shape["group"], mesh.shape["fsdp"]),
        mesh=mesh,
        in_specs=placed,
        out_specs=P(("group", "fsdp"), "ctx", None),
        check_vma=False,
    )
```

```python
import functools

import jax
import jax.numpy as jnp
import numpy as np
from jax import lax
from jax.experimental import pallas as pl
from jax.experimental.pallas import tpu as pltpu
from jax.sharding import PartitionSpec as P

HEAD_DIM = 128
GROUP = 8
THETA = 500000.0
MASKED = -1e30
MESH = pl.DeviceIdType.MESH
PHASES = 2
OUT_GROUPS = 4


def rotary_tables(length):
    half = HEAD_DIM // 2
    exponent = -np.arange(half, dtype=np.float32) * np.float32(2.0) / np.float32(HEAD_DIM)
    frequency = np.power(np.float32(THETA), exponent, dtype=np.float32)
    angles = np.arange(length, dtype=np.float32)[:, None] * frequency[None, :]
    cosine, sine = np.cos(angles).astype(np.float32), np.sin(angles).astype(np.float32)
    return np.concatenate([cosine, cosine], 1), np.concatenate([-sine, sine], 1)


def kernel(
    groups, shards, doc_ref, normed_ref, queries_ref, key_ref, value_ref, cos_hbm, sin_hbm, out_ref,
    wbuf, xbuf, qbuf, obuf, pbuf, inverse, acc, kbuf, vbuf, bias, cos_ref, sin_ref,
    load_sem, recv_sem, z_sem, y_sem, x_sem, pair_send, pair_recv, out_sem, out_send, out_recv,
):
    twins = groups == 2
    ny = 2 if twins else 1
    nz = shards // ny
    parts = 4 if twins else 1
    zparts = 3 if twins else 1
    g, f, c = lax.axis_index("group"), lax.axis_index("fsdp"), lax.axis_index("ctx")
    z, y = f // ny, f % ny
    own_rows, depth = normed_ref.shape[1], key_ref.shape[0]
    length = 2 * own_rows
    piece_rows = depth // parts
    half_cols = queries_ref.shape[2] // 2
    pair = (g, f, 1 - c)
    up, down = (g, f + ny, c), (g, f - ny, c)
    if twins:
        y_dev, x_dev = (g, z * 2 + 1 - y, c), (1 - g, f, c)

    def shard(zs, ys):
        return zs * ny + ys

    def part(j):
        return g * (parts - 1) + j * (1 - 2 * g) if twins else 0

    def piece(h, s, q):
        return wbuf.at[h, s, pl.ds(pl.multiple_of(q * piece_rows, piece_rows), piece_rows), :]

    def copy(h, s, q, send_sem, device):
        ref = piece(h, s, q)
        return pltpu.make_async_remote_copy(
            src_ref=ref, dst_ref=ref, send_sem=send_sem, recv_sem=recv_sem.at[h, s, q],
            device_id=device, device_id_type=MESH,
        )

    def z_copy(h, zs, j, way):
        q = part(j)
        return copy(h, shard(zs, y), q, z_sem.at[way, h, zs, j], up if way == 0 else down)

    def y_copy(h, zs, j):
        return copy(h, shard(zs, y), part(j), y_sem.at[h, zs, j], y_dev)

    def x_copy(h, zs, ys, j, slot):
        return copy(h, shard(zs, ys), part(j), x_sem.at[h, zs, slot], x_dev)

    def wait_piece(h, s, j):
        q = part(j)
        copy(h, s, q, recv_sem.at[h, s, q], pair).wait_recv()

    head_cols = pl.ds(pl.multiple_of(c * 2 * HEAD_DIM, 2 * HEAD_DIM), 2 * HEAD_DIM)
    weight_loads = [
        pltpu.make_async_copy(ref.at[:, head_cols], wbuf.at[h, f], load_sem.at[h])
        for h, ref in enumerate((key_ref, value_ref))
    ]
    own = pl.ds(pl.multiple_of(c * own_rows, own_rows), own_rows)
    other = pl.ds(pl.multiple_of((1 - c) * own_rows, own_rows), own_rows)
    my_cols = pl.ds(pl.multiple_of(c * half_cols, half_cols), half_cols)
    other_cols = pl.ds(pl.multiple_of((1 - c) * half_cols, half_cols), half_cols)
    other_loads = [
        pltpu.make_async_copy(normed_ref.at[0], xbuf.at[own, :], load_sem.at[2]),
        pltpu.make_async_copy(queries_ref.at[0, :, my_cols], qbuf.at[own, :], load_sem.at[3]),
        pltpu.make_async_copy(cos_hbm, cos_ref, load_sem.at[4]),
        pltpu.make_async_copy(sin_hbm, sin_ref, load_sem.at[5]),
    ]
    for load in weight_loads:
        load.start()

    barrier = pltpu.get_barrier_semaphore()
    pl.semaphore_signal(barrier, inc=1, device_id=pair, device_id_type=MESH)
    if twins:
        pl.semaphore_signal(barrier, inc=1, device_id=y_dev, device_id_type=MESH)
        pl.semaphore_signal(barrier, inc=1, device_id=x_dev, device_id_type=MESH)

    @pl.when(z < nz - 1)
    def _():
        pl.semaphore_signal(barrier, inc=1, device_id=up, device_id_type=MESH)

    @pl.when(z > 0)
    def _():
        pl.semaphore_signal(barrier, inc=1, device_id=down, device_id_type=MESH)

    line_peers = jnp.where(z > 0, 1, 0) + jnp.where(z < nz - 1, 1, 0)
    pl.semaphore_wait(barrier, (3 if twins else 1) + line_peers)

    def sends_beside(h, j):
        return twins and (h != 0 or j != 3)

    def send_own(h):
        weight_loads[h].wait()
        for j in range(parts):
            if j < zparts:
                @pl.when(z < nz - 1)
                def _():
                    z_copy(h, z, j, 0).start()

                @pl.when(z > 0)
                def _():
                    z_copy(h, z, j, 1).start()
            if sends_beside(h, j):
                y_copy(h, z, j).start()

    def each_way(d, action):
        @pl.when(z - d >= 0)
        def _():
            action(z - d, 0)

        @pl.when(z + d < nz)
        def _():
            action(z + d, 1)

    def passes_on(way):
        return z < nz - 1 if way == 0 else z > 0

    def forward_z(h, d, some=None):
        for j in range(zparts) if some is None else some:
            def one(zs, way, j=j):
                wait_piece(h, shard(zs, y), j)

                @pl.when(passes_on(way))
                def _():
                    z_copy(h, zs, j, way).start()

                if twins:
                    if j < 2:
                        y_copy(h, zs, j).start()
                    if j == 0:
                        x_copy(h, zs, y, 0, 0).start()

            each_way(d, one)

    def forward_y(h, d):
        for j in range(2):
            def one(zs, way, j=j):
                wait_piece(h, shard(zs, 1 - y), j)
                x_copy(h, zs, 1 - y, j, 1 + j).start()

            each_way(d, one)

    def drain_sends(h, d):
        def one(zs, way):
            for j in range(zparts):
                @pl.when(passes_on(way))
                def _():
                    z_copy(h, zs, j, way).wait_send()

            if twins:
                for j in range(2):
                    y_copy(h, zs, j).wait_send()
                    x_copy(h, zs, 1 - y, j, 1 + j).wait_send()
                x_copy(h, zs, y, 0, 0).wait_send()

        each_way(d, one)

    def drain_own(h):
        for j in range(parts):
            if j < zparts:
                @pl.when(z < nz - 1)
                def _():
                    z_copy(h, z, j, 0).wait_send()

                @pl.when(z > 0)
                def _():
                    z_copy(h, z, j, 1).wait_send()
            if sends_beside(h, j):
                y_copy(h, z, j).wait_send()
        if twins and h == 0:
            x_copy(h, z, 1 - y, 0, 0).wait_send()

    def add_shard(h, s):
        columns = pl.ds(pl.multiple_of(s * depth, depth), depth)

        def tile(t, carry):
            rows = pl.ds(pl.multiple_of(t * 256, 256), 256)
            acc[h, rows, :] += jnp.dot(xbuf[rows, columns], wbuf[h, s], preferred_element_type=jnp.float32)
            return carry

        lax.fori_loop(0, length // 256, tile, 0)

    def add_same(h, d):
        def one(zs, way):
            if twins:
                wait_piece(h, shard(zs, y), 3)
            add_shard(h, shard(zs, y))

        each_way(d, one)

    def add_other(h, d):
        def one(zs, way):
            for j in range(2, 4):
                wait_piece(h, shard(zs, 1 - y), j)
            add_shard(h, shard(zs, 1 - y))

        each_way(d, one)

    def forward_beside():
        wait_piece(0, shard(z, 1 - y), 0)
        x_copy(0, z, 1 - y, 0, 0).start()

    def add_beside(h):
        for j in range(1 if h == 0 else 0, 4):
            wait_piece(h, shard(z, 1 - y), j)
        add_shard(h, shard(z, 1 - y))

    def rotated(u, rows):
        return (u * cos_ref[rows, :] + pltpu.roll(u, HEAD_DIM // 2, 1) * sin_ref[rows, :]).astype(jnp.bfloat16)

    def rotate_queries():
        for load in other_loads[1:]:
            load.wait()
        query_copy.wait_recv()

        def head(i, carry):
            cols = pl.ds(pl.multiple_of(i * HEAD_DIM, HEAD_DIM), HEAD_DIM)

            def tile(t, carry):
                rows = pl.ds(pl.multiple_of(t * 128, 128), 128)
                qbuf[rows, cols] = rotated(qbuf[rows, cols].astype(jnp.float32), rows)
                return carry

            return lax.fori_loop(0, length // 128, tile, carry)

        lax.fori_loop(0, half_cols // HEAD_DIM, head, 0)

    def make_bias():
        first = doc_ref[0]
        row = lax.broadcasted_iota(jnp.int32, (length, length), 0)
        col = lax.broadcasted_iota(jnp.int32, (length, length), 1)
        visible = (col <= row) & ((col >= first) | (row < first))
        bias[...] = jnp.where(visible, 0.0, MASKED)

    def finish_keys():
        def tile(t, carry):
            rows = pl.ds(pl.multiple_of(t * 128, 128), 128)
            for h in range(2):
                kbuf[h, rows, :] = rotated(acc[0, rows, h * HEAD_DIM:(h + 1) * HEAD_DIM], rows)
            return carry

        lax.fori_loop(0, length // 128, tile, 0)

    factor = HEAD_DIM ** -0.5 * 1.4426950408889634

    def weigh(first, count):
        h = first // GROUP

        def head(i, carry):
            cols = pl.ds(pl.multiple_of(i * HEAD_DIM, HEAD_DIM), HEAD_DIM)
            for block in range(2):
                rows = slice(block * own_rows, (block + 1) * own_rows)
                keys = (block + 1) * own_rows
                scores = lax.dot_general(
                    qbuf[rows, cols], kbuf[h, :keys, :], (((1,), (1,)), ((), ())),
                    preferred_element_type=jnp.float32,
                ) * factor + bias[rows, :keys]
                probs = jnp.exp2(scores - jnp.max(scores, axis=1, keepdims=True))
                total = jnp.sum(probs, axis=1, keepdims=True)
                pbuf[i, rows, :keys] = probs.astype(jnp.bfloat16)
                inverse[i, rows, :] = jnp.broadcast_to(1.0 / total, (own_rows, HEAD_DIM))
            return carry

        lax.fori_loop(first, first + count, head, 0)

    def mix(first, count):
        h = first // GROUP

        def head(i, carry):
            cols = pl.ds(pl.multiple_of(i * HEAD_DIM, HEAD_DIM), HEAD_DIM)
            for block in range(2):
                rows = slice(block * own_rows, (block + 1) * own_rows)
                keys = (block + 1) * own_rows
                mixed = jnp.dot(
                    pbuf[i, rows, :keys], vbuf[:keys, h * HEAD_DIM:(h + 1) * HEAD_DIM],
                    preferred_element_type=jnp.float32,
                )
                obuf[rows, cols] = (mixed * inverse[i, rows, :]).astype(jnp.bfloat16)
            return carry

        lax.fori_loop(first, first + count, head, 0)

    def out_copies(h):
        width = half_cols // OUT_GROUPS
        source = pl.ds(h * width, width)
        target = out_ref.at[0, :, pl.ds(pl.multiple_of(c * half_cols + h * width, width), width)]
        return (
            pltpu.make_async_copy(obuf.at[own, source], target, out_sem.at[h]),
            pltpu.make_async_remote_copy(
                src_ref=obuf.at[other, source], dst_ref=target, send_sem=out_send.at[h],
                recv_sem=out_recv.at[h], device_id=pair, device_id_type=MESH,
            ),
        )

    def send_out(h):
        for one in out_copies(h):
            one.start()

    send_own(0)
    query_copy = pltpu.make_async_remote_copy(
        src_ref=queries_ref.at[0, :, other_cols], dst_ref=qbuf.at[own, :], send_sem=pair_send.at[0],
        recv_sem=pair_recv.at[0], device_id=pair, device_id_type=MESH,
    )
    normed_copy = pltpu.make_async_remote_copy(
        src_ref=normed_ref.at[0], dst_ref=xbuf.at[own, :], send_sem=pair_send.at[1],
        recv_sem=pair_recv.at[1], device_id=pair, device_id_type=MESH,
    )
    for load in other_loads:
        load.start()
    query_copy.start()
    normed_copy.start()
    acc[...] = jnp.zeros_like(acc)
    make_bias()

    def wait_normed():
        other_loads[0].wait()
        normed_copy.wait_recv()

    if twins:
        forward_z(0, 1)
        rotate_queries()
        forward_beside()
        forward_z(0, 2)
        forward_y(0, 1)
        send_own(1)
        forward_y(0, 2)
        forward_z(0, 3)
        wait_normed()
        add_shard(0, f)
        add_beside(0)
        add_same(0, 1)
        forward_y(0, 3)
        add_same(0, 2)
        add_other(0, 1)
        forward_z(1, 1)
        add_same(0, 3)
        add_other(0, 2)
        add_other(0, 3)
        finish_keys()
        weigh(0, 2)
        forward_z(1, 2, [0])
        weigh(2, 2)
        forward_z(1, 2, [1])
        weigh(4, 2)
        forward_z(1, 2, [2])
        weigh(6, 2)
        forward_y(1, 1)
        add_shard(1, f)
        add_beside(1)
        weigh(8, 1)
        forward_z(1, 3, [0])
        weigh(9, 2)
        add_same(1, 1)
        forward_z(1, 3, [1])
        weigh(11, 2)
        add_other(1, 1)
        forward_y(1, 2)
        forward_z(1, 3, [2])
        weigh(13, 2)
        add_same(1, 2)
        forward_y(1, 3)
        weigh(15, 1)
        add_other(1, 2)
        add_same(1, 3)
        add_other(1, 3)
    else:
        rotate_queries()
        send_own(1)
        wait_normed()
        for h in range(PHASES):
            add_shard(h, f)

            def step(d, carry, h=h):
                forward_z(h, d)
                add_same(h, d)
                return carry

            lax.fori_loop(1, nz, step, 0)
            if h == 0:
                finish_keys()
                weigh(0, 8)
                weigh(8, 8)
    vbuf[...] = acc[1].astype(jnp.bfloat16)
    heads = 2 * GROUP // OUT_GROUPS
    for group in range(OUT_GROUPS):
        mix(group * heads, heads)
        send_out(group)

    for h in range(PHASES):
        drain_own(h)

        def drain(d, carry, h=h):
            drain_sends(h, d)
            return carry

        lax.fori_loop(1, nz, drain, 0)
    query_copy.wait_send()
    normed_copy.wait_send()
    for group in range(OUT_GROUPS):
        local, remote = out_copies(group)
        local.wait()
        remote.wait()


def body(groups, shards, normed, queries, key_weight, value_weight, doc_start):
    _, rows, width = normed.shape
    depth = key_weight.shape[0]
    query_cols = queries.shape[2]
    length = 2 * rows
    nz = shards // 2 if groups == 2 else shards
    parts = 4 if groups == 2 else 1
    cosine, sine = rotary_tables(length)
    dma = pltpu.SemaphoreType.DMA
    hbm = pl.BlockSpec(memory_space=pltpu.HBM)
    return pl.pallas_call(
        functools.partial(kernel, groups, shards),
        out_shape=jax.ShapeDtypeStruct((1, rows, query_cols), jnp.bfloat16),
        in_specs=[pl.BlockSpec(memory_space=pltpu.SMEM)] + [hbm] * 6,
        out_specs=pl.BlockSpec(memory_space=pl.ANY),
        scratch_shapes=[
            pltpu.VMEM((PHASES, shards, depth, 2 * HEAD_DIM), jnp.bfloat16),
            pltpu.VMEM((length, width), jnp.bfloat16),
            pltpu.VMEM((length, query_cols // 2), jnp.bfloat16),
            pltpu.VMEM((length, query_cols // 2), jnp.bfloat16),
            pltpu.VMEM((2 * GROUP, length, length), jnp.bfloat16),
            pltpu.VMEM((2 * GROUP, length, HEAD_DIM), jnp.float32),
            pltpu.VMEM((PHASES, length, 2 * HEAD_DIM), jnp.float32),
            pltpu.VMEM((2, length, HEAD_DIM), jnp.bfloat16),
            pltpu.VMEM((length, 2 * HEAD_DIM), jnp.bfloat16),
            pltpu.VMEM((length, length), jnp.float32),
            pltpu.VMEM((length, HEAD_DIM), jnp.float32),
            pltpu.VMEM((length, HEAD_DIM), jnp.float32),
            dma((6,)),
            dma((PHASES, shards, parts)),
            dma((2, PHASES, nz, 3)),
            dma((PHASES, nz, 4)),
            dma((PHASES, nz, 3)),
            dma((2,)),
            dma((2,)),
            dma((OUT_GROUPS,)),
            dma((OUT_GROUPS,)),
            dma((OUT_GROUPS,)),
        ],
        compiler_params=pltpu.CompilerParams(
            collective_id=0, has_side_effects=True, vmem_limit_bytes=48 * 1024 * 1024
        ),
    )(doc_start, normed, queries, key_weight, value_weight, jnp.asarray(cosine), jnp.asarray(sine))


def solution(mesh):
    placed = (
        P(("group", "fsdp"), "ctx", None),
        P(("group", "fsdp"), "ctx", None),
        P("fsdp", None),
        P("fsdp", None),
        P(("group", "fsdp")),
    )
    return jax.shard_map(
        functools.partial(body, mesh.shape["group"], mesh.shape["fsdp"]),
        mesh=mesh,
        in_specs=placed,
        out_specs=P(("group", "fsdp"), "ctx", None),
        check_vma=False,
    )
```
